32 devices in a mesh: region: 8 (over z, x), mp: 4 (over y, core).
Axes of the slice: x: 2, y: 2, z: 4, core: 2. Of those that a mesh axis runs over, the one named last changes fastest.
Arguments:
- tokens: bfloat16 [8192, 1024], P('region', 'mp'), may hold values from -6 to 6
- cotangent: bfloat16 [8192, 1024], P('region', 'mp'), may hold values from -6 to 6
- gain: float32 [1024], replicated, may hold values from 0.1 to 1.9
- w_up: bfloat16 [1024, 4096], P(None, 'mp'), may hold values from -0.1875 to 0.1875
- w_down: bfloat16 [4096, 1024], P('mp'), may hold values from -0.09375 to 0.09375
- counts: int32 [32], P('region'), may hold values from 16 to 256, as said below
Outputs:
- d_tokens: bfloat16 [8192, 1024], P('region', 'mp')
- d_up: float32 [1024, 4096], P('region', 'mp')
- d_down: float32 [4096, 1024], P('mp', 'region')
- d_gain: float32 [1024], P('mp')
The draws below stay inside these ranges and needn't reach their ends.
Inputs may be any that keep to these rules, and one draw needn't show every extreme that they name: `counts`: each count is 16 times 1 + 3k for a whole k. Every group of 16 consecutive regions holds 1984 tokens, so all regions hold 3968 tokens together. The 4 regions of one owner hold at most 1024 tokens, and some owner holds exactly 1024 in every draw.
All inputs are finite; a program needn't handle non-finite values.
Results may differ from the reference program's by a relative error of at most 0.015.
Values may be sent and summed in bfloat16 or wider, within the bound.
No kernel may reach another device: no remote copies, remote signals or barrier semaphores. Data moves between devices by JAX's collectives and lax.ppermute only.
A program may use at most 64 MiB of HBM per device.

```python
import math
import jax
import jax.numpy as jnp
from jax import lax

D = 1024
FF = 4096
TILE = 16
REG_DEV = 4
CAP = 1024
BAL = 496
REGIONS = 32
TOTAL = 3968
N_REGION = 8
N_MP = 4


def one_order(subkey):
    return jax.random.permutation(subkey, 16)


def draw_counts(key, part):
    groups = REGIONS // 16
    subkeys = jax.random.split(jax.random.fold_in(key, 11), groups)
    orders = jax.vmap(one_order)(subkeys)
    inverse = jnp.argsort(orders, axis=1, stable=True)
    packets = jnp.array([15, 15, 15, 15, 15, 15, 15, 3] + [0] * 8, dtype=jnp.int32)
    extras = jnp.take(packets, inverse)
    full_group = jax.random.randint(jax.random.fold_in(key, 12), (), 0, groups)
    heavy_owner = jax.random.randint(jax.random.fold_in(key, 13), (), 0, 4)
    slot_owner = jnp.arange(16, dtype=jnp.int32) // 4
    heavy_slot = slot_owner == heavy_owner
    other_slot = jnp.logical_not(heavy_slot)
    other_rank = jnp.cumsum(other_slot.astype(jnp.int32)) - 1
    rest_table = jnp.array([15, 15, 15, 3] + [0] * 12, dtype=jnp.int32)
    rest = jnp.take(rest_table, jnp.clip(other_rank, 0, 15))
    filled = jnp.where(heavy_slot, 15, jnp.where(other_slot, rest, 0)).astype(jnp.int32)
    chosen = (jnp.arange(groups, dtype=jnp.int32) == full_group)[:, None]
    extras = jnp.where(chosen, filled[None, :], extras)
    return (TILE * (1 + extras)).reshape(REGIONS).astype(jnp.int32)


def steps_of(key, extent, pieces, low, top_value):
    def one(axis_at, parts):
        draws = jax.random.uniform(jax.random.fold_in(jax.random.fold_in(key, 6), axis_at), (parts,), jnp.float32, low / len(pieces), top_value / len(pieces))
        return jnp.repeat(jnp.exp(draws), extent[axis_at] // parts).reshape((-1,) + (1,) * (len(extent) - axis_at - 1))

    factor_of = one(*pieces[0])
    for cut in pieces[1:]:
        factor_of = factor_of * one(*cut)
    return factor_of


def noise(own_key, dims, scale, most, cuts=(), kind=jnp.bfloat16):
    result = jax.random.normal(own_key, dims, jnp.float32) * scale
    if len(cuts) > 0:
        result = steps_of(own_key, dims, cuts, -0.22, 0.18) * result
    return jnp.clip(result, min=-most, max=most).astype(kind)


def setup_inputs(seed: int = 0) -> dict:
    splits = jax.random.split(jax.random.key(seed), 7)
    return {
        "tokens": noise(splits[0], (N_REGION * CAP, D), 1.0, 6.0, ((0, 8), (1, 4))),
        "cotangent": noise(splits[1], (N_REGION * CAP, D), 1.0, 6.0, ((0, 8), (1, 4))),
        "gain": jnp.clip(1.0 + 0.18 * jax.random.normal(splits[2], (D,), jnp.float32), 0.1, 1.9),
        "w_up": noise(splits[3], (D, FF), D ** -0.5, 0.1875, ((1, 4),)),
        "w_down": noise(splits[4], (FF, D), FF ** -0.5, 0.09375, ((0, 4),)),
        "counts": draw_counts(jax.random.fold_in(splits[6], 71), 0),
    }


EPSILON = 1e-05

def gelu_tanh(inputs):
    return jax.nn.gelu(inputs, approximate=True)

def reference(tokens, cotangent, gain, w_up, w_down, counts):
    all_loads = lax.optimization_barrier(jnp.sum(counts.reshape(N_REGION, REG_DEV), axis=1)).astype(jnp.int32)
    load_ends = jnp.cumsum(all_loads).astype(jnp.int32)
    load_starts = load_ends - all_loads
    places = jnp.arange(TOTAL, dtype=jnp.int32)
    owner_index = lax.optimization_barrier(jnp.sum((load_ends[None, :] <= places[:, None]).astype(jnp.int32), axis=1)).astype(jnp.int32)
    owner_start = jnp.take(load_starts, owner_index)
    flat_index = (owner_index * CAP + places - owner_start).astype(jnp.int32)
    rows_x = jnp.take(tokens, flat_index, axis=0).reshape(N_REGION, BAL, D)
    rows_dy = jnp.take(cotangent, flat_index, axis=0).reshape(N_REGION, BAL, D)
    group_width = FF // N_MP

    def layer_block(totals, block_item):
        block_x, block_dy = block_item
        whole_float = block_x.astype(jnp.float32)
        inv_rms = lax.rsqrt(lax.optimization_barrier(jnp.mean(whole_float * whole_float, axis=1)) + EPSILON)
        normed = (whole_float * inv_rms[:, None] * gain).astype(jnp.bfloat16)
        hidden = jnp.dot(normed, w_up, preferred_element_type=jnp.float32)
        activated, gelu_back = jax.vjp(gelu_tanh, hidden)
        act_rows = activated.astype(jnp.bfloat16)
        d_act = jnp.dot(block_dy, w_down.T, preferred_element_type=jnp.float32)
        d_hidden = gelu_back(d_act)[0].astype(jnp.bfloat16)
        grouped_h = d_hidden.astype(jnp.float32).reshape(BAL, N_MP, group_width)
        grouped_w = w_up.astype(jnp.float32).reshape(D, N_MP, group_width)
        partial_term = jnp.einsum('rmf,dmf->mrd', grouped_h, grouped_w)
        rounded = lax.optimization_barrier(partial_term.astype(jnp.bfloat16))
        d_normed = lax.optimization_barrier(jnp.sum(rounded.astype(jnp.float32), axis=0))
        weighted = gain * d_normed
        row_dot = lax.optimization_barrier(jnp.sum(weighted * whole_float, axis=1))
        cubed = inv_rms * inv_rms * inv_rms
        d_rows = block_dy.astype(jnp.float32) + weighted * inv_rms[:, None] - whole_float * (row_dot * cubed / D)[:, None]
        up_total, down_total, gain_total = totals
        up_total = up_total + jnp.dot(normed.T, d_hidden, preferred_element_type=jnp.float32)
        down_total = down_total + jnp.dot(act_rows.T, block_dy, preferred_element_type=jnp.float32)
        gain_total = gain_total + lax.optimization_barrier(jnp.sum(d_normed * whole_float * inv_rms[:, None], axis=0))
        return ((up_total, down_total, gain_total), d_rows.astype(jnp.bfloat16))
    start_totals = (jnp.zeros((D, FF), jnp.float32), jnp.zeros((FF, D), jnp.float32), jnp.zeros((D,), jnp.float32))
    totals, d_rows = lax.scan(layer_block, start_totals, (rows_x, rows_dy))
    grad_scale = 1.0 / math.sqrt(TOTAL)
    d_tokens = jnp.zeros((N_REGION * CAP, D), jnp.bfloat16).at[flat_index].set(d_rows.reshape(TOTAL, D))
    return (d_tokens, totals[0] * grad_scale, totals[1] * grad_scale, totals[2] * grad_scale)
```

```python
import math

import jax
import jax.numpy as jnp
from jax import lax
from jax.sharding import PartitionSpec as P

BAL = 496

EPSILON = 1e-05
C0 = math.sqrt(2.0 / math.pi)
C1 = 0.044715


def gelu_and_slope(v):
    square = v * v
    t = jnp.tanh(C0 * v * (1.0 + C1 * square))
    half = 0.5 * (1.0 + t)
    slope = half + 0.5 * v * (1.0 - t * t) * (C0 * (1.0 + 3.0 * C1 * square))
    return v * half, slope


def swap(value, axis, distance, size):
    return lax.ppermute(value, axis, [(i, i ^ distance) for i in range(size)])


def gather_pieces(own, mp_n):
    pieces = [None] * mp_n
    pieces[0] = own
    for j in range(2, mp_n, 2):
        pieces[j] = swap(own, "mp", j, mp_n)
    for j in range(0, mp_n, 2):
        pieces[j + 1] = swap(pieces[j], "mp", 1, mp_n)
    return pieces


def halves(piece, side):
    width = piece.shape[1] // 2
    return (
        lax.dynamic_slice_in_dim(piece, (1 - side) * width, width, axis=1),
        lax.dynamic_slice_in_dim(piece, side * width, width, axis=1),
    )


def ordered(pieces, side):
    split = [halves(p, side) for p in pieces]
    return jnp.concatenate([s for s, _ in split] + [k for _, k in split], axis=1)


def ordered_rows(weight, place, side, mp_n):
    block = weight.shape[0] // mp_n
    width = block // 2
    parts = []
    for h in (1 - side, side):
        for j in range(mp_n):
            start = (place ^ j) * block + h * width
            parts.append(lax.dynamic_slice_in_dim(weight, start, width, axis=0))
    return jnp.concatenate(parts, axis=0)


def ordered_columns(weight, place, side, mp_n):
    block = weight.shape[1] // mp_n
    width = block // 2
    parts = []
    for h in (1 - side, side):
        for j in range(mp_n):
            start = (place ^ j) * block + h * width
            parts.append(lax.dynamic_slice_in_dim(weight, start, width, axis=1))
    return jnp.concatenate(parts, axis=1)


def on_device(tokens, cotangent, gain, w_up, w_down, counts):
    regions_n = lax.axis_size("region")
    mp_n = lax.axis_size("mp")
    rows_cap, share = tokens.shape
    features = gain.shape[0]
    units = w_up.shape[1]
    scale = 1.0 / math.sqrt(BAL * regions_n)
    r = lax.axis_index("region")
    place = lax.axis_index("mp")
    side = r % 2
    tier = r // 2
    tiers = regions_n // 2
    if tiers != mp_n:
        raise ValueError("mesh shape")
    f32, bf16 = jnp.float32, jnp.bfloat16

    live = (jnp.arange(rows_cap, dtype=jnp.int32) < jnp.sum(counts)).astype(f32)[:, None]
    gain_p = ordered_columns(gain[None, :], place, side, mp_n)
    up_p = ordered_rows(w_up, place, side, mp_n)
    down_p = ordered_columns(w_down, place, side, mp_n)

    x_pieces = gather_pieces(tokens, mp_n)
    y_pieces = gather_pieces(cotangent, mp_n)

    squares = sum(jnp.sum(jnp.square(p.astype(f32)), axis=1, keepdims=True) for p in x_pieces)
    inv = lax.rsqrt(squares / features + EPSILON)
    x_p = ordered(x_pieces, side)
    normed = (x_p.astype(f32) * inv * gain_p).astype(bf16)
    hidden = jnp.dot(normed, up_p, preferred_element_type=f32)
    act, slope = gelu_and_slope(hidden)
    act = (act * live).astype(bf16)
    slope = slope * live

    y_p = ordered(y_pieces, side)
    middle = features // 2

    def outer(left, right):
        return lax.dot_general(left, right, (((0,), (0,)), ((), ())), preferred_element_type=f32) * scale

    cuts = 2
    step = units // cuts
    spans = [slice(i * step, (i + 1) * step) for i in range(cuts)]

    d_act = lax.dot_general(y_p, down_p, (((1,), (1,)), ((), ())), preferred_element_type=f32)
    d_hidden = (d_act * slope).astype(bf16)

    work = [(y_p, act[:, s]) for s in spans] + [(normed, d_hidden[:, s]) for s in spans]
    received = []
    for left, right in work:
        first = outer(left[:, :middle], right).astype(bf16)
        received.append(swap(first, "region", 1, regions_n))

    term = lax.dot_general(d_hidden, up_p, (((1,), (1,)), ((), ())), preferred_element_type=f32)
    dot_term = jnp.sum(term * normed.astype(f32), axis=1)
    term = term.astype(bf16)

    finals = []
    for (left, right), got in zip(work, received):
        total = (outer(left[:, middle:], right) + got.astype(f32)).astype(bf16)
        blocks = total.reshape(tiers, share // 2, step)
        out = lax.dynamic_index_in_dim(blocks, place ^ tier, keepdims=False).astype(f32)
        for k in range(1, tiers):
            part = lax.dynamic_index_in_dim(blocks, place ^ tier ^ k, keepdims=False)
            out = out + swap(part, "region", 2 * k, regions_n).astype(f32)
        finals.append(out)

    def piece(j):
        w = share // 2
        return jnp.concatenate([term[:, j * w : (j + 1) * w], term[:, middle + j * w : middle + (j + 1) * w]], axis=1)

    near = {}
    for j in range(0, mp_n, 2):
        near[j] = (piece(j).astype(f32) + swap(piece(j + 1), "mp", 1, mp_n).astype(f32))
    d_normed = near[0]
    for j in range(2, mp_n, 2):
        d_normed = d_normed + swap(near[j].astype(bf16), "mp", j, mp_n).astype(f32)
    row_dot = dot_term
    j = 1
    while j < mp_n:
        row_dot = row_dot + swap(row_dot, "mp", j, mp_n)
        j *= 2

    w = share // 2
    d_normed = jnp.where(
        side == 1, d_normed, jnp.concatenate([d_normed[:, w:], d_normed[:, :w]], axis=1)
    )
    own_gain = lax.dynamic_slice_in_dim(gain, place * share, share)[None, :]
    x_own = tokens.astype(f32)
    gain_term = jnp.sum(d_normed * x_own * (inv * live), axis=0) * scale
    j = 1
    while j < regions_n:
        gain_term = gain_term + swap(gain_term, "region", j, regions_n)
        j *= 2
    d_rows = cotangent.astype(f32) + inv * (own_gain * d_normed - x_own * (row_dot[:, None] * (inv / features)))
    d_rows = jnp.where(live > 0, d_rows, 0.0)
    d_down = jnp.concatenate(finals[:cuts], axis=1).T
    d_up = jnp.concatenate(finals[cuts:], axis=1)
    return d_rows.astype(bf16), d_up, d_down, gain_term


def solution(mesh):
    placed = (P("region", "mp"), P("region", "mp"), P(), P(None, "mp"), P("mp", None), P("region"))
    return jax.shard_map(
        on_device,
        mesh=mesh,
        in_specs=placed,
        out_specs=(P("region", "mp"), P("region", "mp"), P("mp", "region"), P("mp")),
        check_vma=False,
    )
```

```python
import functools
import math

import jax
import jax.numpy as jnp
from jax import lax
from jax.experimental import pallas as pl
from jax.experimental.pallas import tpu as pltpu
from jax.sharding import PartitionSpec as P

BAL = 496

EPSILON = 1e-05
C0 = math.sqrt(2.0 / math.pi)
C1 = 0.044715
F32, BF16 = jnp.float32, jnp.bfloat16
LANES = 128


def gelu_and_slope(v):
    square = v * v
    t = jnp.tanh(C0 * v * (1.0 + C1 * square))
    half = 0.5 * (1.0 + t)
    slope = half + 0.5 * v * (1.0 - t * t) * (C0 * (1.0 + 3.0 * C1 * square))
    return v * half, slope


def swap(value, axis, distance, size):
    return lax.ppermute(value, axis, [(i, i ^ distance) for i in range(size)])


class Line:
    def __init__(self):
        self.last = None

    def __call__(self, value):
        if self.last is None:
            return value
        value, _ = lax.optimization_barrier((value, self.last))
        return value

    def mark(self, value):
        self.last = value
        return value


def chunk_keys(n):
    bits = n.bit_length() - 1
    return [sum((1 - ((p >> (bits - 1 - i)) & 1)) << i for i in range(bits)) for p in range(n)]


def pack_weights(w_up, w_down, gain, by_region, by_place):
    features, units = w_up.shape
    n = features // LANES

    def body(a, b, up1, up2, down, g, up1_o, up2_o, down_o, g_o):
        up1_o[...] = up1[...]
        up2_o[...] = up2[...]
        down_o[...] = down[...]
        g_o[...] = g[0]

    return pl.pallas_call(
        body,
        grid_spec=pltpu.PrefetchScalarGridSpec(
            num_scalar_prefetch=2,
            grid=(n,),
            in_specs=[
                pl.BlockSpec((LANES, units), lambda p, a, b: (a[p], 0)),
                pl.BlockSpec((LANES, units), lambda p, a, b: (b[p], 0)),
                pl.BlockSpec((units, LANES), lambda p, a, b: (0, a[p])),
                pl.BlockSpec((1, 1, LANES), lambda p, a, b: (a[p], 0, 0)),
            ],
            out_specs=[
                pl.BlockSpec((LANES, units), lambda p, a, b: (p, 0)),
                pl.BlockSpec((LANES, units), lambda p, a, b: (p, 0)),
                pl.BlockSpec((units, LANES), lambda p, a, b: (0, p)),
                pl.BlockSpec((1, LANES), lambda p, a, b: (0, p)),
            ],
        ),
        out_shape=[
            jax.ShapeDtypeStruct((features, units), BF16),
            jax.ShapeDtypeStruct((features, units), BF16),
            jax.ShapeDtypeStruct((units, features), BF16),
            jax.ShapeDtypeStruct((1, features), F32),
        ],
        cost_estimate=pl.CostEstimate(flops=0, transcendentals=0, bytes_accessed=12 * features * units),
        name="pack_weights",
    )(by_region, by_place, w_up, w_up, w_down, gain.reshape(n, 1, LANES))


def norm_rows(pieces, gain_p, spots):
    rows, share = pieces[0].shape
    features = share * len(pieces)
    halves = share // LANES
    tile = 256

    def body(spot, gain_ref, *refs):
        ins, normed, inv_ref = refs[: len(pieces)], refs[-2], refs[-1]
        total = jnp.zeros((tile, LANES), F32)
        for ref in ins:
            for h in range(halves):
                v = ref[:, h * LANES : (h + 1) * LANES].astype(F32)
                total = total + v * v
        inv = lax.rsqrt(jnp.sum(total, axis=1, keepdims=True) / features + EPSILON)
        inv_ref[...] = jnp.broadcast_to(inv, (tile, LANES))
        for j, ref in enumerate(ins):
            for h in range(halves):
                at = pl.ds(pl.multiple_of(spot[j * halves + h] * LANES, LANES), LANES)
                v = ref[:, h * LANES : (h + 1) * LANES].astype(F32)
                normed[:, at] = (v * inv * gain_ref[:, at]).astype(BF16)

    return pl.pallas_call(
        body,
        grid_spec=pltpu.PrefetchScalarGridSpec(
            num_scalar_prefetch=1,
            grid=(rows // tile,),
            in_specs=[pl.BlockSpec((1, features), lambda i, s: (0, 0))]
            + [pl.BlockSpec((tile, share), lambda i, s: (i, 0))] * len(pieces),
            out_specs=[
                pl.BlockSpec((tile, features), lambda i, s: (i, 0)),
                pl.BlockSpec((tile, LANES), lambda i, s: (i, 0)),
            ],
        ),
        out_shape=[jax.ShapeDtypeStruct((rows, features), BF16), jax.ShapeDtypeStruct((rows, LANES), F32)],
        cost_estimate=pl.CostEstimate(flops=4 * rows * features, transcendentals=rows, bytes_accessed=4 * rows * features),
        name="norm_rows",
    )(spots, gain_p, *pieces)


def pack_rows(pieces, spots):
    rows, share = pieces[0].shape
    features = share * len(pieces)
    halves = share // LANES
    tile = 256

    def body(spot, *refs):
        ins, out = refs[: len(pieces)], refs[-1]
        for j, ref in enumerate(ins):
            for h in range(halves):
                at = pl.ds(pl.multiple_of(spot[j * halves + h] * LANES, LANES), LANES)
                out[:, at] = ref[:, h * LANES : (h + 1) * LANES]

    return pl.pallas_call(
        body,
        grid_spec=pltpu.PrefetchScalarGridSpec(
            num_scalar_prefetch=1,
            grid=(rows // tile,),
            in_specs=[pl.BlockSpec((tile, share), lambda i, s: (i, 0))] * len(pieces),
            out_specs=pl.BlockSpec((tile, features), lambda i, s: (i, 0)),
        ),
        out_shape=jax.ShapeDtypeStruct((rows, features), BF16),
        cost_estimate=pl.CostEstimate(flops=0, transcendentals=0, bytes_accessed=4 * rows * features),
        name="pack_rows",
    )(spots, *pieces)


def take_chunks(array, order, axis, width):
    parts = [lax.dynamic_slice_in_dim(array, order[p] * width, width, axis=axis) for p in range(order.shape[0])]
    return jnp.concatenate(parts, axis=axis)


def on_device(tokens, cotangent, gain, w_up, w_down, counts):
    regions_n = lax.axis_size("region")
    mp_n = lax.axis_size("mp")
    rows_cap, share = tokens.shape
    features = gain.shape[0]
    units = w_up.shape[1]
    scale = 1.0 / math.sqrt(BAL * regions_n)
    r = lax.axis_index("region")
    place = lax.axis_index("mp")
    chunk = features // regions_n
    per_piece = share // chunk
    aligned = chunk == LANES and share % LANES == 0 and rows_cap % 256 == 0

    keys = chunk_keys(regions_n)
    by_region = r ^ jnp.array(keys, jnp.int32)
    inverse = [0] * regions_n
    for p, key in enumerate(keys):
        inverse[key] = p
    spans = jnp.arange(regions_n, dtype=jnp.int32)
    by_place = (place ^ (spans // per_piece)) * per_piece + spans % per_piece
    spots = jnp.take(jnp.array(inverse, jnp.int32), by_place ^ r)

    def far_pieces(own):
        return {j: (own if j == 0 else swap(own, "mp", j, mp_n)) for j in range(0, mp_n, 2)}

    def all_pieces(far):
        out = []
        for j in range(0, mp_n, 2):
            out += [far[j], swap(far[j], "mp", 1, mp_n)]
        return out

    x_pieces = all_pieces(far_pieces(tokens))
    y_pieces = all_pieces(far_pieces(cotangent))

    live = (jnp.arange(rows_cap, dtype=jnp.int32) < jnp.sum(counts)).astype(F32)[:, None]
    if aligned:
        up_p, up_m, down_p, gain_p = pack_weights(w_up, w_down, gain, by_region, by_place)
        normed, inv = norm_rows(x_pieces, gain_p, spots)
        inv = inv[:, :1]
        y_p = pack_rows(y_pieces, spots)
    else:
        up_p = take_chunks(w_up, by_region, 0, chunk)
        up_m = take_chunks(w_up, by_place, 0, chunk)
        down_p = take_chunks(w_down, by_region, 1, chunk)
        whole = jnp.concatenate(x_pieces, axis=1).astype(F32)
        inv = lax.rsqrt(jnp.sum(whole * whole, axis=1, keepdims=True) / features + EPSILON)
        by_spot = jnp.argsort(spots)
        normed = take_chunks((whole * inv * take_chunks(gain[None, :], by_place, 1, chunk)).astype(BF16), by_spot, 1, chunk)
        y_p = take_chunks(jnp.concatenate(y_pieces, axis=1), by_spot, 1, chunk)

    hidden = jnp.dot(normed, up_p, preferred_element_type=F32)
    act, slope = gelu_and_slope(hidden)
    act = (act * live).astype(BF16)
    slope = slope * live

    line = Line()
    middle = features // 2
    bits = regions_n.bit_length() - 1

    class Block:
        def __init__(self, kind, left, right):
            self.kind, self.left, self.right = kind, left, right
            self.got = []
            self.start = 0

        def piece(self, width):
            at, self.start = self.start, self.start + width
            cols = line(self.left)[:, at : at + width]
            if self.kind == "up":
                out = lax.dot_general(cols, self.right, (((0,), (0,)), ((), ())), preferred_element_type=F32)
            else:
                out = lax.dot_general(self.right, cols, (((0,), (0,)), ((), ())), preferred_element_type=F32)
            out = out * scale
            for begin, got in self.got:
                if self.kind == "up":
                    out = out + got[at - begin : at - begin + width].astype(F32)
                else:
                    out = out + got[:, at - begin : at - begin + width].astype(F32)
            return out

        def step(self, bit):
            width = (features - self.start) // 2
            first = line.mark(self.piece(width).astype(BF16))
            self.got.append((self.start, swap(first, "region", 1 << bit, regions_n)))

        def last(self):
            self.result = line.mark(self.piece(chunk))

    cuts = 2 if units % 256 == 0 else 1
    width = units // cuts
    parts = [slice(i * width, (i + 1) * width) for i in range(cuts)]
    downs = [Block("down", y_p, act[:, s]) for s in parts]
    for b in downs:
        b.step(0)
    d_act = lax.dot_general(line(y_p), down_p, (((1,), (1,)), ((), ())), preferred_element_type=F32)
    d_hidden = line.mark((d_act * slope).astype(BF16))
    ups = [Block("up", normed, d_hidden[:, s]) for s in parts]
    for b in ups:
        b.step(0)
    term = lax.dot_general(line(d_hidden), up_m, (((1,), (1,)), ((), ())), preferred_element_type=F32)
    term = line.mark(term.astype(BF16))
    passed = {j: swap(term[:, (j + 1) * share : (j + 2) * share], "mp", 1, mp_n) for j in range(0, mp_n, 2)}

    blocks = downs + ups
    near = {}
    d_normed = None

    def pair_sums():
        kept = line(term)
        for j in range(0, mp_n, 2):
            value = kept[:, j * share : (j + 1) * share].astype(F32) + passed[j].astype(F32)
            near[j] = value if j == 0 else swap(line.mark(value.astype(BF16)), "mp", j, mp_n).astype(F32)

    for i, b in enumerate(blocks):
        b.step(1)
        if i == 0:
            pair_sums()
        for bit in range(2, bits):
            b.step(bit)
            if bit == 2 and i > 0:
                blocks[i - 1].last()
    blocks[-1].last()

    d_normed = sum(near[j] for j in range(0, mp_n, 2))
    own_gain = lax.dynamic_slice_in_dim(gain, place * share, share)[None, :]
    x_own = tokens.astype(F32)
    weighted = own_gain * d_normed
    row_dot = jnp.sum(weighted * x_own, axis=1)
    j = 1
    while j < mp_n:
        row_dot = row_dot + swap(row_dot, "mp", j, mp_n)
        j *= 2
    gain_term = jnp.sum(d_normed * x_own * (inv * live), axis=0) * scale
    j = 1
    while j < regions_n:
        gain_term = gain_term + swap(gain_term, "region", j, regions_n)
        j *= 2
    d_rows = cotangent.astype(F32) + weighted * inv - x_own * (row_dot[:, None] * (inv * inv * inv / features))
    d_rows = jnp.where(live > 0, d_rows, 0.0)
    d_down = jnp.concatenate([b.result for b in downs], axis=0)
    d_up = jnp.concatenate([b.result for b in ups], axis=1)
    return d_rows.astype(BF16), d_up, d_down, gain_term


def solution(mesh):
    placed = (P("region", "mp"), P("region", "mp"), P(), P(None, "mp"), P("mp", None), P("region"))
    return jax.shard_map(
        on_device,
        mesh=mesh,
        in_specs=placed,
        out_specs=(P("region", "mp"), P("region", "mp"), P("mp", "region"), P("mp")),
        check_vma=False,
    )
```
